32 devices in a mesh: section: 16 (over z, x, core), chan: 2 (over y).
Axes of the slice: x: 2, y: 2, z: 4, core: 2. Of those that a mesh axis runs over, the one named last changes fastest.
Arguments:
- voltages: bfloat16 [128, 2048, 2048], P('section', 'chan'), may hold values from -6 to 6
- fir_taps: float32 [4, 2048], replicated, may hold values from -1 to 1
- steer: float32 [32, 2048], replicated, may hold values from -0.05 to 0.05
- beam_dir: int32 [1024], replicated, may hold values from 0 to 31
- input_order: int32 [2048], replicated, may hold values from 0 to 2047, each once
Outputs:
- vis: bfloat16 [32, 2048, 2048], P(('section', 'chan'))
- beams: bfloat16 [32, 2, 1024, 128], P(('section', 'chan'))
The draws below stay inside these ranges and needn't reach their ends.
Inputs may be any that keep to these rules, and one draw needn't show every extreme that they name: `input_order`: each of 0 to 2047 once.
All inputs are finite; a program needn't handle non-finite values.
Results may differ from the reference program's by a relative error of at most 0.0058.
Values may be sent and summed in bfloat16 or wider, within the bound.
No kernel may reach another device: no remote copies, remote signals or barrier semaphores. Data moves between devices by JAX's collectives and lax.ppermute only.
A program may use at most 192 MiB of HBM per device.

```python
import math
import jax
import jax.numpy as jnp
from jax import lax

NI = 2048
FRAME = 2048
TAPS = 4
NB = 1024
NDIR = 32
STOT = 128
CH = 32
FIRST = 256


def set_ends(drawn, stream_key, low, top_value):
    dims = drawn.shape
    spot = [jax.random.randint(jax.random.fold_in(stream_key, axis), (), 0, dims[axis]) for axis in range(len(dims))]
    drawn = drawn.at[tuple(spot)].set(low)
    longest = dims.index(max(dims))
    spot[longest] = (spot[longest] + 1) % dims[longest]
    return drawn.at[tuple(spot)].set(top_value)


def shard_levels(key, shape, split, least, high):
    loudness = 1.0
    for dim, shards_of in split:
        draws = jax.random.uniform(jax.random.fold_in(jax.random.fold_in(key, 6), dim), (shards_of,), jnp.float32, least / len(split), high / len(split))
        loudness = loudness * jnp.repeat(jnp.exp(draws), shape[dim] // shards_of).reshape((-1,) + (1,) * (len(shape) - 1 - dim))
    return loudness


def centred(own_key, dims, width, bound, cuts=(), kind=jnp.bfloat16):
    loudness = shard_levels(own_key, dims, cuts, -0.22, 0.18) if cuts else 1.0
    drawn = jax.random.normal(own_key, dims, jnp.float32) * width * loudness
    return jnp.minimum(jnp.maximum(drawn, -bound), bound).astype(kind)


def setup_inputs(seed: int = 0) -> dict:
    arg_keys = jax.random.split(jax.random.key(seed), 6)
    voltages = centred(arg_keys[0], (STOT, NI, FRAME), 1.0, 6.0, ((0, 16), (1, 2)))
    fir_taps = jnp.clip(jax.random.uniform(arg_keys[1], (TAPS, FRAME), jnp.float32, -1.0, 1.0), -1.0, 1.0)
    steer = jnp.clip(jax.random.uniform(arg_keys[2], (NDIR, NI), jnp.float32, -0.05, 0.05), -0.05, 0.05)
    beam_dir = set_ends(jax.random.randint(arg_keys[3], (NB,), 0, NDIR), jax.random.fold_in(arg_keys[3], 1), 0, NDIR - 1).astype(jnp.int32)
    input_order = jax.random.permutation(arg_keys[4], NI).astype(jnp.int32)
    return {"voltages": voltages, "fir_taps": fir_taps, "steer": steer, "beam_dir": beam_dir, "input_order": input_order}


def input_spectra(block, fir_taps):
    count = block.shape[1]
    frames = jnp.transpose(block, (1, 0, 2)).astype(jnp.float32)
    padded = jnp.concatenate([jnp.zeros((count, TAPS - 1, FRAME), jnp.float32), frames], axis=1)
    filtered = jnp.zeros((count, STOT, FRAME), jnp.float32)
    for tap_index in range(TAPS):
        offset = TAPS - 1 - tap_index
        filtered = filtered + fir_taps[tap_index][None, None, :] * padded[:, offset:offset + STOT, :]
    spectrum = jnp.fft.rfft(filtered, axis=-1)[:, :, FIRST:FIRST + CH] / math.sqrt(FRAME)
    real_part = jnp.real(spectrum).astype(jnp.bfloat16)
    imag_part = jnp.imag(spectrum).astype(jnp.bfloat16)
    return jnp.transpose(jnp.stack([real_part, imag_part], axis=0), (3, 0, 1, 2))

def channel_products(spectrum, channel, steer, beam_dir, input_order):
    ordered = jnp.take(spectrum, input_order, axis=1)
    real_part = ordered[0]
    imag_part = ordered[1]
    re_vis = jnp.dot(real_part, real_part.T, preferred_element_type=jnp.float32) + jnp.dot(imag_part, imag_part.T, preferred_element_type=jnp.float32)
    im_vis = jnp.dot(imag_part, real_part.T, preferred_element_type=jnp.float32) - jnp.dot(real_part, imag_part.T, preferred_element_type=jnp.float32)
    row_index = lax.broadcasted_iota(jnp.int32, (NI, NI), 0)
    col_index = lax.broadcasted_iota(jnp.int32, (NI, NI), 1)
    vis = (jnp.where(col_index >= row_index, re_vis, im_vis) * (1.0 / math.sqrt(STOT))).astype(jnp.bfloat16)
    frequency = (FIRST + channel).astype(jnp.float32)
    phase = jnp.take(steer, beam_dir, axis=0) * frequency
    w_real = (jnp.cos(phase) / math.sqrt(NI)).astype(jnp.bfloat16)
    w_imag = (-jnp.sin(phase) / math.sqrt(NI)).astype(jnp.bfloat16)
    beam_real = jnp.dot(w_real, real_part, preferred_element_type=jnp.float32) - jnp.dot(w_imag, imag_part, preferred_element_type=jnp.float32)
    beam_imag = jnp.dot(w_real, imag_part, preferred_element_type=jnp.float32) + jnp.dot(w_imag, real_part, preferred_element_type=jnp.float32)
    beams = jnp.stack([beam_real, beam_imag], axis=0).astype(jnp.bfloat16)
    return (vis, beams)

def reference(voltages, fir_taps, steer, beam_dir, input_order):
    block_rows = min(128, NI)
    blocks = jnp.transpose(voltages.reshape(STOT, NI // block_rows, block_rows, FRAME), (1, 0, 2, 3))
    spectra = lax.map(lambda block: input_spectra(block, fir_taps), blocks)
    spectra = jnp.transpose(spectra, (1, 2, 0, 3, 4)).reshape(CH, 2, NI, STOT)
    channels = jnp.arange(CH, dtype=jnp.int32)
    vis, beams = lax.map(lambda item: channel_products(item[0], item[1], steer, beam_dir, input_order), (spectra, channels))
    return (vis, beams)
```

```python
import functools
import math

import jax
import jax.numpy as jnp
import numpy as np
from jax import lax
from jax.experimental import pallas as pl
from jax.experimental.pallas import tpu as pltpu
from jax.sharding import PartitionSpec as P

MINOR = (((1,), (1,)), ((), ()))
MAJOR = (((0,), (0,)), ((), ()))
VMEM_BYTES = 56 << 20
LANES = 128


def fourier_table(frame, first, channels):
    turns = np.arange(first, first + channels)[:, None] * np.arange(frame)[None, :] % frame
    angle = turns * (2.0 * math.pi / frame)
    factor = 1.0 / math.sqrt(frame)
    pair = np.stack([np.cos(angle) * factor, -np.sin(angle) * factor], axis=1)
    return pair.reshape(2 * channels, frame).astype(np.float32)


def frame_products(frames, taps, volts_ref, wave_ref, fir_ref, held, table, sems, block, emit):
    rows = wave_ref.shape[0]
    blocks = volts_ref.shape[1] // block
    count = len(frames)

    def copy(b, k):
        start = pl.multiple_of(b * block, block)
        return pltpu.make_async_copy(
            volts_ref.at[frames[k], pl.ds(start, block)],
            held.at[b * count + k],
            sems.at[b * count + k],
        )

    for b in range(blocks):
        for k in range(count):
            copy(b, k).start()
    for m in range(taps):
        table[m * rows : (m + 1) * rows, :] = (wave_ref[...] * fir_ref[m : m + 1, :]).astype(
            table.dtype
        )

    def body(b, carry):
        sums = {}
        for k in range(count):
            copy(b, k).wait()
            terms = lax.dot_general(
                table[...], held[b * count + k], MINOR, preferred_element_type=jnp.float32
            )
            for m in range(taps):
                part = terms[m * rows : (m + 1) * rows]
                at = frames[k] + m
                sums[at] = sums[at] + part if at in sums else part
        emit(pl.ds(pl.multiple_of(b * block, block), block), sums)
        return carry

    lax.fori_loop(0, blocks, body, 0)


def last_frames_kernel(
    total, taps, block, volts_ref, wave_ref, fir_ref, own_ref, tail_ref, held, table, sems
):
    lag = taps - 1

    def emit(at, sums):
        for k in range(lag):
            own_ref[k, :, at] = sums[total - lag + k]
            tail_ref[k, :, at] = sums[total + k].astype(tail_ref.dtype)

    frames = list(range(total - lag, total))
    frame_products(frames, taps, volts_ref, wave_ref, fir_ref, held, table, sems, block, emit)


def first_frames_kernel(
    total, taps, block, volts_ref, wave_ref, fir_ref, own_ref, sum_ref, held, table, sems
):
    lag = taps - 1

    def emit(at, sums):
        for t in range(total):
            value = sums[t]
            if t >= total - lag:
                value = value + own_ref[t - (total - lag), :, at]
            sum_ref[t, :, at] = value

    frames = list(range(total - lag))
    frame_products(frames, taps, volts_ref, wave_ref, fir_ref, held, table, sems, block, emit)


def join_kernel(sum_ref, carried_ref, out_ref, rows):
    total, count = sum_ref.shape[0], sum_ref.shape[1]
    lag = carried_ref.shape[0]
    for t in range(total):
        value = sum_ref[t]
        if t < lag:
            value = value + carried_ref[t].astype(jnp.float32)
        for j in range(rows.shape[0]):
            rows[j, pl.ds(t, count, stride=total), :] = value[:, j * LANES : (j + 1) * LANES]
    for j in range(rows.shape[0]):
        out_ref[:, j * LANES : (j + 1) * LANES] = rows[j].astype(out_ref.dtype)


def channel_kernel(
    scale, got_ref, order_ref, weight_ref, dir_ref, vis_ref, beam_ref, flat, mixed, turned
):
    sections, chans, pair, inputs = got_ref.shape
    frames = sections * pair // 2
    total = flat.shape[1]
    block = vis_ref.shape[0]
    step = pl.program_id(0)

    @pl.when(step == 0)
    def _():
        for c in range(chans):
            flat[:, c * inputs : (c + 1) * inputs] = got_ref[:, c].reshape(2 * frames, inputs)
        for start in range(0, total, block):
            source = lax.broadcasted_iota(jnp.int32, (total, block), 0)
            chosen = (source == order_ref[:, start : start + block]).astype(jnp.bfloat16)
            picked = jnp.dot(flat[...], chosen, preferred_element_type=jnp.float32)
            parts = picked.reshape(sections, 2, pair // 2, block)
            real = parts[:, 0].reshape(frames, block)
            imag = parts[:, 1].reshape(frames, block)
            mixed[:, start : start + block] = jnp.concatenate([real, imag], axis=0).astype(
                mixed.dtype
            )
            turned[:, start : start + block] = jnp.concatenate([-imag, real], axis=0).astype(
                turned.dtype
            )
        both = lax.dot_general(
            weight_ref[...], mixed[...], MINOR, preferred_element_type=jnp.float32
        )
        dirs = both.shape[0] // 2
        beam_real = both[:dirs, :frames] - both[dirs:, frames:]
        beam_imag = both[:dirs, frames:] + both[dirs:, :frames]
        formed = jnp.concatenate([beam_real, beam_imag], axis=1).astype(jnp.bfloat16)
        beams = beam_ref.shape[1]
        row = lax.broadcasted_iota(jnp.int32, (dirs, beams), 0)
        chosen = (row == dir_ref[...]).astype(jnp.bfloat16)
        spread = lax.dot_general(chosen, formed, MAJOR, preferred_element_type=jnp.float32)
        beam_ref[0] = spread[:, :frames].astype(beam_ref.dtype)
        beam_ref[1] = spread[:, frames:].astype(beam_ref.dtype)

    here = pl.ds(pl.multiple_of(step * block, block), block)
    left = mixed[:, here]
    products = lax.dot_general(left, mixed[...], MAJOR, preferred_element_type=jnp.float32)
    vis_ref[...] = (products * scale).astype(vis_ref.dtype)
    other = turned[:, here]
    real = lax.dot_general(left, left, MAJOR, preferred_element_type=jnp.float32)
    imag = lax.dot_general(left, other, MAJOR, preferred_element_type=jnp.float32)
    row = lax.broadcasted_iota(jnp.int32, (block, block), 0)
    col = lax.broadcasted_iota(jnp.int32, (block, block), 1)
    vis_ref[:, here] = (jnp.where(col >= row, real, imag) * scale).astype(vis_ref.dtype)
    mixed[:, here] = other


def on_device(voltages, fir_taps, steer, beam_dir, input_order):
    section_count = lax.axis_size("section")
    chan_count = lax.axis_size("chan")
    devices = section_count * chan_count
    spec_dev, inputs_here, frame = voltages.shape
    taps = fir_taps.shape[0]
    lag = taps - 1
    channels = devices
    first = frame // 8
    rows = 2 * channels
    total_inputs = inputs_here * chan_count
    total_frames = spec_dev * section_count
    wave = jnp.asarray(fourier_table(frame, first, channels))
    block = min(256, inputs_here)
    blocks = inputs_here // block
    whole = pl.BlockSpec(memory_space=pltpu.VMEM)

    def call(kernel, frames, extra, outs):
        return pl.pallas_call(
            functools.partial(kernel, spec_dev, taps, block),
            in_specs=[pl.BlockSpec(memory_space=pl.ANY)] + [whole] * (2 + len(extra)),
            out_specs=[whole] * len(outs),
            out_shape=outs,
            scratch_shapes=[
                pltpu.VMEM((frames * blocks, block, frame), voltages.dtype),
                pltpu.VMEM((taps * rows, frame), jnp.bfloat16),
                pltpu.SemaphoreType.DMA((frames * blocks,)),
            ],
            compiler_params=pltpu.CompilerParams(vmem_limit_bytes=VMEM_BYTES),
            cost_estimate=pl.CostEstimate(
                flops=2 * taps * rows * frame * inputs_here * frames,
                bytes_accessed=2 * frame * inputs_here * frames,
                transcendentals=0,
            ),
        )(voltages, wave, fir_taps, *extra)

    own, tail = call(
        last_frames_kernel,
        lag,
        (),
        [
            jax.ShapeDtypeStruct((lag, rows, inputs_here), jnp.float32),
            jax.ShapeDtypeStruct((lag, rows, inputs_here), jnp.bfloat16),
        ],
    )
    carried = lax.ppermute(tail, "section", [(i, i + 1) for i in range(section_count - 1)])
    (sums,) = call(
        first_frames_kernel,
        spec_dev - lag,
        (own,),
        [jax.ShapeDtypeStruct((spec_dev, rows, inputs_here), jnp.float32)],
    )
    spectra = pl.pallas_call(
        join_kernel,
        in_specs=[whole] * 2,
        out_specs=whole,
        out_shape=jax.ShapeDtypeStruct((rows * spec_dev, inputs_here), jnp.bfloat16),
        scratch_shapes=[pltpu.VMEM((inputs_here // LANES, rows * spec_dev, LANES), jnp.float32)],
        compiler_params=pltpu.CompilerParams(vmem_limit_bytes=VMEM_BYTES),
    )(sums, carried)
    got = lax.all_to_all(
        spectra.reshape(devices, 2 * spec_dev, inputs_here),
        ("section", "chan"),
        split_axis=0,
        concat_axis=0,
        tiled=True,
    ).reshape(section_count, chan_count, 2 * spec_dev, inputs_here)

    channel = lax.axis_index("section") * chan_count + lax.axis_index("chan")
    phase = steer * (first + channel).astype(jnp.float32)
    size = math.sqrt(total_inputs)
    weights = jnp.concatenate([jnp.cos(phase) / size, -jnp.sin(phase) / size], axis=0).astype(
        jnp.bfloat16
    )
    beam_count = beam_dir.shape[0]
    vis_rows = min(256, total_inputs)
    fixed = lambda shape: pl.BlockSpec(shape, lambda i: (0,) * len(shape))
    vis, beams = pl.pallas_call(
        functools.partial(channel_kernel, 1.0 / math.sqrt(total_frames)),
        grid=(total_inputs // vis_rows,),
        in_specs=[
            fixed(got.shape),
            fixed((1, total_inputs)),
            fixed(weights.shape),
            fixed((1, beam_count)),
        ],
        out_specs=[
            pl.BlockSpec((vis_rows, total_inputs), lambda i: (i, 0)),
            fixed((2, beam_count, total_frames)),
        ],
        out_shape=[
            jax.ShapeDtypeStruct((total_inputs, total_inputs), jnp.bfloat16),
            jax.ShapeDtypeStruct((2, beam_count, total_frames), jnp.bfloat16),
        ],
        scratch_shapes=[
            pltpu.VMEM((2 * total_frames, total_inputs), jnp.bfloat16),
            pltpu.VMEM((2 * total_frames, total_inputs), jnp.bfloat16),
            pltpu.VMEM((2 * total_frames, total_inputs), jnp.bfloat16),
        ],
        compiler_params=pltpu.CompilerParams(vmem_limit_bytes=VMEM_BYTES),
    )(got, input_order.reshape(1, total_inputs), weights, beam_dir.reshape(1, beam_count))
    return (vis[None], beams[None])


def solution(mesh):
    return jax.shard_map(
        on_device,
        mesh=mesh,
        in_specs=(P("section", "chan", None), P(), P(), P(), P()),
        out_specs=(P(("section", "chan"), None, None), P(("section", "chan"), None, None, None)),
        check_vma=False,
    )
```

```python
import functools
import math

import jax
import jax.numpy as jnp
import numpy as np
from jax import lax
from jax.experimental import pallas as pl
from jax.experimental.pallas import tpu as pltpu
from jax.sharding import PartitionSpec as P

MINOR = (((1,), (1,)), ((), ()))
MAJOR = (((0,), (0,)), ((), ()))
LANES = 128
AHEAD = 8


def fourier_table(frame, first, channels):
    turns = np.arange(first, first + channels)[:, None] * np.arange(frame)[None, :] % frame
    angle = turns * (2.0 * math.pi / frame)
    factor = 1.0 / math.sqrt(frame)
    pair = np.stack([np.cos(angle) * factor, -np.sin(angle) * factor], axis=1)
    return pair.reshape(2 * channels, frame).astype(np.float32)


def frame_products(frames, taps, volts_ref, table, held, sems, block, prepare, emit):
    rows = table.shape[0] // taps
    inputs = volts_ref.shape[1]
    count = len(frames)
    unit = block // 2 if block % (2 * LANES) == 0 else block
    per = block // unit
    copies = []
    for start in range(0, inputs, block):
        for k in range(count):
            for at in range(start, start + block, unit):
                place = len(copies)
                copies.append(
                    pltpu.make_async_copy(
                        volts_ref.at[frames[k], pl.ds(at, unit)],
                        held.at[k, pl.ds(at, unit)],
                        sems.at[place],
                    )
                )
    for copy in copies[:AHEAD]:
        copy.start()
    prepare()
    done = 0
    for start in range(0, inputs, block):
        sums = {}
        for k in range(count):
            for copy in copies[done : done + per]:
                copy.wait()
            for copy in copies[done + AHEAD : done + AHEAD + per]:
                copy.start()
            done += per
            terms = lax.dot_general(
                table[...],
                held[k, start : start + block],
                MINOR,
                preferred_element_type=jnp.float32,
            )
            for m in range(taps):
                part = terms[m * rows : (m + 1) * rows]
                at = frames[k] + m
                sums[at] = sums[at] + part if at in sums else part
        emit(slice(start, start + block), sums)


def last_frames_kernel(
    total, taps, block, volts_ref, wave_hbm, fir_hbm, own_ref, tail_ref, table, held, sems,
    wave, fir, extra,
):
    lag = taps - 1
    rows = wave.shape[0]
    loads = [
        pltpu.make_async_copy(wave_hbm, wave, extra.at[0]),
        pltpu.make_async_copy(fir_hbm, fir, extra.at[1]),
    ]
    for load in loads:
        load.start()

    def prepare():
        for load in loads:
            load.wait()
        for m in range(taps):
            table[m * rows : (m + 1) * rows, :] = (wave[...] * fir[m : m + 1, :]).astype(table.dtype)

    def emit(at, sums):
        for k in range(lag):
            own_ref[k, :, at] = sums[total - lag + k]
            tail_ref[k, :, at] = sums[total + k].astype(tail_ref.dtype)

    frames = list(range(total - lag, total))
    frame_products(frames, taps, volts_ref, table, held, sems, block, prepare, emit)


def first_frames_kernel(total, taps, block, volts_ref, table_ref, own_ref, sum_ref, held, sems):
    lag = taps - 1

    def emit(at, sums):
        for t in range(total):
            value = sums[t]
            if t >= total - lag:
                value = value + own_ref[t - (total - lag), :, at]
            sum_ref[t, :, at] = value

    frames = list(range(total - lag))
    frame_products(frames, taps, volts_ref, table_ref, held, sems, block, lambda: None, emit)


def join_kernel(sum_ref, carried_ref, out_ref, rows):
    total, count = sum_ref.shape[0], sum_ref.shape[1]
    lag = carried_ref.shape[0]
    for t in range(total):
        value = sum_ref[t]
        if t < lag:
            value = value + carried_ref[t].astype(jnp.float32)
        for j in range(rows.shape[0]):
            rows[j, pl.ds(t, count, stride=total), :] = value[:, j * LANES : (j + 1) * LANES]
    for j in range(rows.shape[0]):
        out_ref[:, j * LANES : (j + 1) * LANES] = rows[j].astype(out_ref.dtype)


def channel_kernel(
    scale, block, got_ref, order_ref, weight_ref, dir_ref, vis_hbm, beam_ref,
    flat, mixed, turned, across, vis, sems,
):
    sections, chans, pair, inputs = got_ref.shape
    frames = sections * pair // 2
    total = flat.shape[1]
    for c in range(chans):
        flat[:, c * inputs : (c + 1) * inputs] = got_ref[:, c].reshape(2 * frames, inputs)
    for start in range(0, total, block):
        at = slice(start, start + block)
        source = lax.broadcasted_iota(jnp.int32, (total, block), 0)
        chosen = (source == order_ref[:, at]).astype(jnp.bfloat16)
        picked = jnp.dot(flat[...], chosen, preferred_element_type=jnp.float32)
        parts = picked.reshape(sections, 2, pair // 2, block)
        real = parts[:, 0].reshape(frames, block)
        imag = parts[:, 1].reshape(frames, block)
        both = jnp.concatenate([real, imag], axis=0).astype(mixed.dtype)
        mixed[:, at] = both
        turned[:, at] = jnp.concatenate([-imag, real], axis=0).astype(turned.dtype)
        across[at, :] = both.T
    copies = []
    for start in range(0, total, block):
        at = slice(start, start + block)
        end = start + block
        above = jnp.dot(across[:end], mixed[:, at], preferred_element_type=jnp.float32)
        below = jnp.dot(across[start:], turned[:, at], preferred_element_type=jnp.float32)
        row = lax.broadcasted_iota(jnp.int32, (block, block), 0)
        col = lax.broadcasted_iota(jnp.int32, (block, block), 1)
        crossing = jnp.where(col >= row, above[start:], below[:block])
        if start > 0:
            vis[:start, at] = (above[:start] * scale).astype(vis.dtype)
        vis[at, at] = (crossing * scale).astype(vis.dtype)
        if end < total:
            vis[end:, at] = (below[block:] * scale).astype(vis.dtype)
        copies.append(pltpu.make_async_copy(vis.at[:, at], vis_hbm.at[:, at], sems.at[len(copies)]))
        copies[-1].start()
    mix = jnp.dot(weight_ref[...], across[...], preferred_element_type=jnp.float32)
    dirs = mix.shape[0] // 2
    beam_real = mix[:dirs, :frames] - mix[dirs:, frames:]
    beam_imag = mix[:dirs, frames:] + mix[dirs:, :frames]
    formed = jnp.concatenate([beam_real, beam_imag], axis=1).astype(jnp.bfloat16)
    beams = beam_ref.shape[1]
    row = lax.broadcasted_iota(jnp.int32, (dirs, beams), 0)
    chosen = (row == dir_ref[...]).astype(jnp.bfloat16)
    spread = lax.dot_general(chosen, formed, MAJOR, preferred_element_type=jnp.float32)
    beam_ref[0] = spread[:, :frames].astype(beam_ref.dtype)
    beam_ref[1] = spread[:, frames:].astype(beam_ref.dtype)
    for copy in copies:
        copy.wait()


def on_device(voltages, fir_taps, steer, beam_dir, input_order):
    section_count = lax.axis_size("section")
    chan_count = lax.axis_size("chan")
    devices = section_count * chan_count
    spec_dev, inputs_here, frame = voltages.shape
    taps = fir_taps.shape[0]
    lag = taps - 1
    channels = devices
    first = frame // 8
    rows = 2 * channels
    total_inputs = inputs_here * chan_count
    total_frames = spec_dev * section_count
    wave = jnp.asarray(fourier_table(frame, first, channels))
    block = min(512, inputs_here)
    whole = pl.BlockSpec(memory_space=pltpu.VMEM)

    stay = pl.BlockSpec(memory_space=pltpu.HBM)

    def call(kernel, frames, operands, specs, outs, scratch):
        held = frames * inputs_here * frame * voltages.dtype.itemsize
        limit = held + 2 * taps * rows * frame * 2 + (12 << 20)
        return pl.pallas_call(
            functools.partial(kernel, spec_dev, taps, block),
            in_specs=specs,
            out_specs=[whole] * len(outs),
            out_shape=outs,
            scratch_shapes=[
                pltpu.VMEM((frames, inputs_here, frame), voltages.dtype),
                pltpu.SemaphoreType.DMA((2 * frames * inputs_here // block,)),
                *scratch,
            ],
            compiler_params=pltpu.CompilerParams(vmem_limit_bytes=limit),
            cost_estimate=pl.CostEstimate(
                flops=2 * taps * rows * frame * inputs_here * frames,
                bytes_accessed=held,
                transcendentals=0,
            ),
        )(*operands)

    keep = lambda x: pltpu.with_memory_space_constraint(x, pltpu.HBM)
    own, tail, table = call(
        last_frames_kernel,
        lag,
        (voltages, keep(wave), keep(fir_taps)),
        [stay, stay, stay],
        [
            jax.ShapeDtypeStruct((lag, rows, inputs_here), jnp.float32),
            jax.ShapeDtypeStruct((lag, rows, inputs_here), jnp.bfloat16),
            jax.ShapeDtypeStruct((taps * rows, frame), jnp.bfloat16),
        ],
        [
            pltpu.VMEM(wave.shape, wave.dtype),
            pltpu.VMEM(fir_taps.shape, fir_taps.dtype),
            pltpu.SemaphoreType.DMA((2,)),
        ],
    )
    carried = lax.ppermute(tail, "section", [(i, i + 1) for i in range(section_count - 1)])
    (sums,) = call(
        first_frames_kernel,
        spec_dev - lag,
        (voltages, table, own),
        [stay, whole, whole],
        [jax.ShapeDtypeStruct((spec_dev, rows, inputs_here), jnp.float32)],
        [],
    )
    spectra = pl.pallas_call(
        join_kernel,
        in_specs=[whole] * 2,
        out_specs=whole,
        out_shape=jax.ShapeDtypeStruct((rows * spec_dev, inputs_here), jnp.bfloat16),
        scratch_shapes=[pltpu.VMEM((inputs_here // LANES, rows * spec_dev, LANES), jnp.float32)],
        compiler_params=pltpu.CompilerParams(vmem_limit_bytes=12 << 20),
    )(sums, carried)
    got = lax.all_to_all(
        spectra.reshape(devices, 2 * spec_dev, inputs_here),
        ("section", "chan"),
        split_axis=0,
        concat_axis=0,
        tiled=True,
    ).reshape(section_count, chan_count, 2 * spec_dev, inputs_here)

    channel = lax.axis_index("section") * chan_count + lax.axis_index("chan")
    phase = steer * (first + channel).astype(jnp.float32)
    size = math.sqrt(total_inputs)
    weights = jnp.concatenate([jnp.cos(phase) / size, -jnp.sin(phase) / size], axis=0).astype(
        jnp.bfloat16
    )
    beam_count = beam_dir.shape[0]
    block = min(256, total_inputs)
    lanes = 2 * total_frames
    vis, beams = pl.pallas_call(
        functools.partial(channel_kernel, 1.0 / math.sqrt(total_frames), block),
        in_specs=[whole] * 4,
        out_specs=[pl.BlockSpec(memory_space=pl.ANY), whole],
        out_shape=[
            jax.ShapeDtypeStruct((total_inputs, total_inputs), jnp.bfloat16),
            jax.ShapeDtypeStruct((2, beam_count, total_frames), jnp.bfloat16),
        ],
        scratch_shapes=[
            pltpu.VMEM((lanes, total_inputs), jnp.bfloat16),
            pltpu.VMEM((lanes, total_inputs), jnp.bfloat16),
            pltpu.VMEM((lanes, total_inputs), jnp.bfloat16),
            pltpu.VMEM((total_inputs, lanes), jnp.bfloat16),
            pltpu.VMEM((total_inputs, total_inputs), jnp.bfloat16),
            pltpu.SemaphoreType.DMA((total_inputs // block,)),
        ],
        compiler_params=pltpu.CompilerParams(vmem_limit_bytes=32 << 20),
    )(got, input_order.reshape(1, total_inputs), weights, beam_dir.reshape(1, beam_count))
    return (vis[None], beams[None])


def solution(mesh):
    return jax.shard_map(
        on_device,
        mesh=mesh,
        in_specs=(P("section", "chan", None), P(), P(), P(), P()),
        out_specs=(P(("section", "chan"), None, None), P(("section", "chan"), None, None, None)),
        check_vma=False,
    )
```

```python
import functools
import math

import jax
import jax.numpy as jnp
from jax import lax
from jax.experimental import pallas as pl
from jax.experimental.pallas import tpu as pltpu
from jax.sharding import PartitionSpec as P

MINOR = (((1,), (1,)), ((), ()))
MAJOR = (((0,), (0,)), ((), ()))
LANES = 128
AHEAD = 4
EARLY = 2


def fourier_rows(frame, first, channels):
    shape = (channels, frame)
    samples = lax.broadcasted_iota(jnp.int32, shape, 1)
    bins = lax.broadcasted_iota(jnp.int32, shape, 0) + first
    quarter = frame // 4
    if frame & (frame - 1):
        turns = lax.rem(bins * samples, frame)
        quadrant = lax.div(turns + quarter // 2, quarter)
    else:
        turns = (bins * samples) & (frame - 1)
        quadrant = (turns + quarter // 2) >> (quarter.bit_length() - 1)
    angle = (turns - quadrant * quarter).astype(jnp.float32) * (2.0 * math.pi / frame)
    square = angle * angle
    sine = 1.0 / 362880.0
    for term in (-1.0 / 5040.0, 1.0 / 120.0, -1.0 / 6.0, 1.0):
        sine = sine * square + term
    sine = sine * angle
    cosine = 1.0 / 40320.0
    for term in (-1.0 / 720.0, 1.0 / 24.0, -0.5, 1.0):
        cosine = cosine * square + term
    factor = 1.0 / math.sqrt(frame)
    odd = (quadrant & 1) == 1
    real = jnp.where(odd, sine, cosine) * jnp.where(((quadrant + 1) & 2) == 2, -factor, factor)
    imag = jnp.where(odd, cosine, sine) * jnp.where((quadrant & 2) == 2, factor, -factor)
    return real, imag


def frame_products(frames, taps, volts_ref, table, held, sems, block, prepare, emit):
    rows = table.shape[0] // taps
    inputs = volts_ref.shape[1]
    count = len(frames)
    unit = block
    per = 1
    copies = []
    for start in range(0, inputs, block):
        for k in range(count):
            for at in range(start, start + block, unit):
                place = len(copies)
                copies.append(
                    pltpu.make_async_copy(
                        volts_ref.at[frames[k], pl.ds(at, unit)],
                        held.at[k, pl.ds(at, unit)],
                        sems.at[place],
                    )
                )
    for copy in copies[:EARLY]:
        copy.start()
    prepare()
    for copy in copies[EARLY:AHEAD]:
        copy.start()
    done = 0
    for start in range(0, inputs, block):
        sums = {}
        for k in range(count):
            for copy in copies[done : done + per]:
                copy.wait()
            for copy in copies[done + AHEAD : done + AHEAD + per]:
                copy.start()
            done += per
            terms = lax.dot_general(
                table[...],
                held[k, start : start + block],
                MINOR,
                preferred_element_type=jnp.float32,
            )
            for m in range(taps):
                part = terms[m * rows : (m + 1) * rows]
                at = frames[k] + m
                sums[at] = sums[at] + part if at in sums else part
        emit(slice(start, start + block), sums)


def last_frames_kernel(
    first, total, taps, block, volts_ref, fir_hbm, own_ref, tail_ref, table, held, sems,
    fir, loaded,
):
    lag = taps - 1
    rows, frame = table.shape[0] // taps, table.shape[1]
    load = pltpu.make_async_copy(fir_hbm, fir, loaded)
    load.start()

    def prepare():
        step = min(rows // 2, 8)
        for start in range(0, rows // 2, step):
            real, imag = fourier_rows(frame, first + start, step)
            if start == 0:
                load.wait()
            for m in range(taps):
                row = fir[m : m + 1, :]
                at = m * rows + start
                table[at : at + step, :] = (real * row).astype(table.dtype)
                at += rows // 2
                table[at : at + step, :] = (imag * row).astype(table.dtype)

    def emit(at, sums):
        for k in range(lag):
            own_ref[k, :, at] = sums[total - lag + k]
            tail_ref[k, :, at] = sums[total + k].astype(tail_ref.dtype)

    frames = list(range(total - lag, total))
    frame_products(frames, taps, volts_ref, table, held, sems, block, prepare, emit)


def first_frames_kernel(total, taps, block, volts_ref, table_ref, own_ref, sum_ref, held, sems):
    lag = taps - 1

    def emit(at, sums):
        for t in range(total):
            value = sums[t]
            if t >= total - lag:
                value = value + own_ref[t - (total - lag), :, at]
            sum_ref[t, :, at] = value

    frames = list(range(total - lag))
    frame_products(frames, taps, volts_ref, table_ref, held, sems, block, lambda: None, emit)


def join_kernel(sum_ref, carried_ref, out_hbm, rows, out, sems):
    total, count = sum_ref.shape[0], sum_ref.shape[1] // 2
    lag = carried_ref.shape[0]
    per = rows.shape[0] // sems.shape[0]
    copies = []
    for j in range(rows.shape[0]):
        at = slice(j * LANES, (j + 1) * LANES)
        for t in range(total):
            value = sum_ref[t, :, at]
            if t < lag:
                value = value + carried_ref[t, :, at].astype(jnp.float32)
            for part in range(2):
                spot = pl.ds(part * total + t, count, stride=2 * total)
                rows[j, spot, :] = value[part * count : (part + 1) * count]
        out[:, at] = rows[j].astype(out.dtype)
        if (j + 1) % per == 0:
            at = slice((j + 1 - per) * LANES, (j + 1) * LANES)
            copies.append(pltpu.make_async_copy(out.at[:, at], out_hbm.at[:, at], sems.at[j // per]))
            copies[-1].start()
    for copy in copies:
        copy.wait()


def channel_kernel(
    scale, block, got_ref, order_ref, weight_ref, dir_ref, vis_hbm, beam_ref,
    flat, mixed, turned, across, vis, sems,
):
    sections, chans, pair, inputs = got_ref.shape
    frames = sections * pair // 2
    total = flat.shape[1]
    for c in range(chans):
        flat[:, c * inputs : (c + 1) * inputs] = got_ref[:, c].reshape(2 * frames, inputs)
    for start in range(0, total, block):
        at = slice(start, start + block)
        source = lax.broadcasted_iota(jnp.int32, (total, block), 0)
        chosen = (source == order_ref[:, at]).astype(jnp.bfloat16)
        picked = jnp.dot(flat[...], chosen, preferred_element_type=jnp.float32)
        parts = picked.reshape(sections, 2, pair // 2, block)
        real = parts[:, 0].reshape(frames, block)
        imag = parts[:, 1].reshape(frames, block)
        both = jnp.concatenate([real, imag], axis=0).astype(mixed.dtype)
        mixed[:, at] = both
        turned[:, at] = jnp.concatenate([-imag, real], axis=0).astype(turned.dtype)
        across[at, :] = both.T
    copies = []
    for start in range(0, total, block):
        at = slice(start, start + block)
        end = start + block
        above = jnp.dot(across[:end], mixed[:, at], preferred_element_type=jnp.float32)
        below = jnp.dot(across[start:], turned[:, at], preferred_element_type=jnp.float32)
        row = lax.broadcasted_iota(jnp.int32, (block, block), 0)
        col = lax.broadcasted_iota(jnp.int32, (block, block), 1)
        crossing = jnp.where(col >= row, above[start:], below[:block])
        if start > 0:
            vis[:start, at] = (above[:start] * scale).astype(vis.dtype)
        vis[at, at] = (crossing * scale).astype(vis.dtype)
        if end < total:
            vis[end:, at] = (below[block:] * scale).astype(vis.dtype)
        copies.append(pltpu.make_async_copy(vis.at[:, at], vis_hbm.at[:, at], sems.at[len(copies)]))
        copies[-1].start()
    mix = jnp.dot(weight_ref[...], across[...], preferred_element_type=jnp.float32)
    dirs = mix.shape[0] // 2
    beam_real = mix[:dirs, :frames] - mix[dirs:, frames:]
    beam_imag = mix[:dirs, frames:] + mix[dirs:, :frames]
    formed = jnp.concatenate([beam_real, beam_imag], axis=1).astype(jnp.bfloat16)
    beams = beam_ref.shape[1]
    row = lax.broadcasted_iota(jnp.int32, (dirs, beams), 0)
    chosen = (row == dir_ref[...]).astype(jnp.bfloat16)
    spread = lax.dot_general(chosen, formed, MAJOR, preferred_element_type=jnp.float32)
    beam_ref[0] = spread[:, :frames].astype(beam_ref.dtype)
    beam_ref[1] = spread[:, frames:].astype(beam_ref.dtype)
    for copy in copies:
        copy.wait()


def on_device(voltages, fir_taps, steer, beam_dir, input_order):
    section_count = lax.axis_size("section")
    chan_count = lax.axis_size("chan")
    devices = section_count * chan_count
    spec_dev, inputs_here, frame = voltages.shape
    taps = fir_taps.shape[0]
    lag = taps - 1
    channels = devices
    first = frame // 8
    rows = 2 * channels
    total_inputs = inputs_here * chan_count
    total_frames = spec_dev * section_count
    block = min(512, inputs_here)
    whole = pl.BlockSpec(memory_space=pltpu.VMEM)

    stay = pl.BlockSpec(memory_space=pltpu.HBM)

    def call(kernel, frames, operands, specs, outs, scratch):
        held = frames * inputs_here * frame * voltages.dtype.itemsize
        limit = held + 2 * taps * rows * frame * 2 + (12 << 20)
        return pl.pallas_call(
            functools.partial(kernel, spec_dev, taps, block),
            in_specs=specs,
            out_specs=[whole] * len(outs),
            out_shape=outs,
            scratch_shapes=[
                pltpu.VMEM((frames, inputs_here, frame), voltages.dtype),
                pltpu.SemaphoreType.DMA((frames * inputs_here // block,)),
                *scratch,
            ],
            compiler_params=pltpu.CompilerParams(vmem_limit_bytes=limit),
            cost_estimate=pl.CostEstimate(
                flops=2 * taps * rows * frame * inputs_here * frames,
                bytes_accessed=held,
                transcendentals=0,
            ),
        )(*operands)

    keep = lambda x: pltpu.with_memory_space_constraint(x, pltpu.HBM)
    own, tail, table = call(
        functools.partial(last_frames_kernel, first),
        lag,
        (voltages, keep(fir_taps)),
        [stay, stay],
        [
            jax.ShapeDtypeStruct((lag, rows, inputs_here), jnp.float32),
            jax.ShapeDtypeStruct((lag, rows, inputs_here), jnp.bfloat16),
            jax.ShapeDtypeStruct((taps * rows, frame), jnp.bfloat16),
        ],
        [
            pltpu.VMEM(fir_taps.shape, fir_taps.dtype),
            pltpu.SemaphoreType.DMA,
        ],
    )
    carried = lax.ppermute(tail, "section", [(i, i + 1) for i in range(section_count - 1)])
    (sums,) = call(
        first_frames_kernel,
        spec_dev - lag,
        (voltages, table, own),
        [stay, whole, whole],
        [jax.ShapeDtypeStruct((spec_dev, rows, inputs_here), jnp.float32)],
        [],
    )
    lane_blocks = inputs_here // LANES
    spectra = pl.pallas_call(
        join_kernel,
        in_specs=[whole] * 2,
        out_specs=pl.BlockSpec(memory_space=pl.ANY),
        out_shape=jax.ShapeDtypeStruct((rows * spec_dev, inputs_here), jnp.bfloat16),
        scratch_shapes=[
            pltpu.VMEM((lane_blocks, rows * spec_dev, LANES), jnp.float32),
            pltpu.VMEM((rows * spec_dev, inputs_here), jnp.bfloat16),
            pltpu.SemaphoreType.DMA((min(4, lane_blocks),)),
        ],
        compiler_params=pltpu.CompilerParams(vmem_limit_bytes=12 << 20),
    )(sums, carried)
    got = lax.all_to_all(
        spectra.reshape(devices, 2 * spec_dev, inputs_here),
        ("section", "chan"),
        split_axis=0,
        concat_axis=0,
        tiled=True,
    ).reshape(section_count, chan_count, 2 * spec_dev, inputs_here)

    channel = lax.axis_index("section") * chan_count + lax.axis_index("chan")
    phase = steer * (first + channel).astype(jnp.float32)
    size = math.sqrt(total_inputs)
    weights = jnp.concatenate([jnp.cos(phase) / size, -jnp.sin(phase) / size], axis=0).astype(
        jnp.bfloat16
    )
    beam_count = beam_dir.shape[0]
    block = min(256, total_inputs)
    lanes = 2 * total_frames
    vis, beams = pl.pallas_call(
        functools.partial(channel_kernel, 1.0 / math.sqrt(total_frames), block),
        in_specs=[whole] * 4,
        out_specs=[pl.BlockSpec(memory_space=pl.ANY), whole],
        out_shape=[
            jax.ShapeDtypeStruct((total_inputs, total_inputs), jnp.bfloat16),
            jax.ShapeDtypeStruct((2, beam_count, total_frames), jnp.bfloat16),
        ],
        scratch_shapes=[
            pltpu.VMEM((lanes, total_inputs), jnp.bfloat16),
            pltpu.VMEM((lanes, total_inputs), jnp.bfloat16),
            pltpu.VMEM((lanes, total_inputs), jnp.bfloat16),
            pltpu.VMEM((total_inputs, lanes), jnp.bfloat16),
            pltpu.VMEM((total_inputs, total_inputs), jnp.bfloat16),
            pltpu.SemaphoreType.DMA((total_inputs // block,)),
        ],
        compiler_params=pltpu.CompilerParams(vmem_limit_bytes=32 << 20),
    )(got, input_order.reshape(1, total_inputs), weights, beam_dir.reshape(1, beam_count))
    return (vis[None], beams[None])


def solution(mesh):
    return jax.shard_map(
        on_device,
        mesh=mesh,
        in_specs=(P("section", "chan", None), P(), P(), P(), P()),
        out_specs=(P(("section", "chan"), None, None), P(("section", "chan"), None, None, None)),
        check_vma=False,
    )
```

```python
import functools
import math

import jax
import jax.numpy as jnp
from jax import lax
from jax.experimental import pallas as pl
from jax.experimental.pallas import tpu as pltpu
from jax.sharding import PartitionSpec as P

MINOR = (((1,), (1,)), ((), ()))
MAJOR = (((0,), (0,)), ((), ()))
GROUP = 8
AHEAD = 4
EARLY = 2
PRE = 1


def fourier_rows(frame, first, channels):
    shape = (channels, frame)
    samples = lax.broadcasted_iota(jnp.int32, shape, 1)
    bins = lax.broadcasted_iota(jnp.int32, shape, 0) + first
    quarter = frame // 4
    if frame & (frame - 1):
        turns = lax.rem(bins * samples, frame)
        quadrant = lax.div(turns + quarter // 2, quarter)
    else:
        turns = (bins * samples) & (frame - 1)
        quadrant = (turns + quarter // 2) >> (quarter.bit_length() - 1)
    angle = (turns - quadrant * quarter).astype(jnp.float32) * (2.0 * math.pi / frame)
    square = angle * angle
    sine = 1.0 / 362880.0
    for term in (-1.0 / 5040.0, 1.0 / 120.0, -1.0 / 6.0, 1.0):
        sine = sine * square + term
    sine = sine * angle
    cosine = 1.0 / 40320.0
    for term in (-1.0 / 720.0, 1.0 / 24.0, -0.5, 1.0):
        cosine = cosine * square + term
    factor = 1.0 / math.sqrt(frame)
    odd = (quadrant & 1) == 1
    real = jnp.where(odd, sine, cosine) * jnp.where(((quadrant + 1) & 2) == 2, -factor, factor)
    imag = jnp.where(odd, cosine, sine) * jnp.where((quadrant & 2) == 2, factor, -factor)
    return real, imag


def frame_products(
    frames, taps, volts_ref, table, held, sems, block, prepare, emit, ready=None, spare=(),
):
    rows = table.shape[0] // taps
    inputs = volts_ref.shape[1]
    count = len(frames)
    have = 0 if ready is None else ready.shape[0]
    unit = block
    per = 1
    copies = []
    for start in range(0, inputs, block):
        for k in range(have, count):
            for at in range(start, start + block, unit):
                place = len(copies)
                copies.append(
                    pltpu.make_async_copy(
                        volts_ref.at[frames[k], pl.ds(at, unit)],
                        held.at[k, pl.ds(at, unit)],
                        sems.at[place],
                    )
                )
    copies += spare
    for copy in copies[:EARLY]:
        copy.start()
    prepare()
    for copy in copies[EARLY:AHEAD]:
        copy.start()
    done = 0
    for start in range(0, inputs, block):
        sums = {}
        for k in range(count):
            if k >= have:
                for copy in copies[done : done + per]:
                    copy.wait()
                for copy in copies[done + AHEAD : done + AHEAD + per]:
                    copy.start()
                done += per
            volts = ready if k < have else held
            terms = lax.dot_general(
                table[...],
                volts[k, start : start + block],
                MINOR,
                preferred_element_type=jnp.float32,
            )
            for m in range(taps):
                part = terms[m * rows : (m + 1) * rows]
                at = frames[k] + m
                sums[at] = sums[at] + part if at in sums else part
        emit(slice(start, start + block), sums)
    for copy in copies[done + AHEAD :]:
        copy.start()
    for copy in copies[done:]:
        copy.wait()


def last_frames_kernel(
    first, total, taps, block, volts_ref, fir_hbm, own_ref, tail_ref, table, next_ref, held, sems,
    fir, loaded, spared,
):
    lag = taps - 1
    rows, frame = table.shape[0] // taps, table.shape[1]
    load = pltpu.make_async_copy(fir_hbm, fir, loaded)
    load.start()

    def prepare():
        step = min(rows // 2, 8)
        for start in range(0, rows // 2, step):
            real, imag = fourier_rows(frame, first + start, step)
            if start == 0:
                load.wait()
            for m in range(taps):
                row = fir[m : m + 1, :]
                at = m * rows + start
                table[at : at + step, :] = (real * row).astype(table.dtype)
                at += rows // 2
                table[at : at + step, :] = (imag * row).astype(table.dtype)

    def emit(at, sums):
        for k in range(lag):
            own_ref[k, :, at] = sums[total - lag + k]
            tail_ref[k, :, at] = sums[total + k].astype(tail_ref.dtype)

    spare = [
        pltpu.make_async_copy(
            volts_ref.at[k, pl.ds(at, block)], next_ref.at[k, pl.ds(at, block)], spared.at[k, i]
        )
        for i, at in enumerate(range(0, volts_ref.shape[1], block))
        for k in range(next_ref.shape[0])
    ]
    frames = list(range(total - lag, total))
    frame_products(
        frames, taps, volts_ref, table, held, sems, block, prepare, emit, spare=spare
    )


def first_frames_kernel(
    total, taps, block, volts_ref, table_ref, own_ref, ready_ref, sum_ref, held, sems
):
    lag = taps - 1

    def emit(at, sums):
        for t in range(total):
            value = sums[t]
            if t >= total - lag:
                value = value + own_ref[t - (total - lag), :, at]
            sum_ref[t, :, at] = value

    frames = list(range(total - lag))
    frame_products(
        frames, taps, volts_ref, table_ref, held, sems, block, lambda: None, emit, ready_ref
    )


def join_kernel(sum_ref, carried_ref, out_hbm, out, sems):
    total, count = sum_ref.shape[0], sum_ref.shape[1] // 2
    lag = carried_ref.shape[0]
    size = 2 * total * GROUP
    shape = (size, size)
    row = lax.broadcasted_iota(jnp.int32, shape, 0)
    col = lax.broadcasted_iota(jnp.int32, shape, 1)
    within = lax.rem(row, 2 * total)
    part, frame = lax.div(within, total), lax.rem(within, total)
    source = (2 * frame + part) * GROUP + lax.div(row, 2 * total)
    move = (source == col).astype(out.dtype)
    copies = []
    for first in range(0, count, GROUP):
        pieces = []
        for t in range(total):
            for p in range(2):
                at = slice(p * count + first, p * count + first + GROUP)
                value = sum_ref[t, at, :]
                if t < lag:
                    value = value + carried_ref[t, at, :].astype(jnp.float32)
                pieces.append(value)
        group = jnp.concatenate(pieces, axis=0).astype(out.dtype)
        at = slice(2 * total * first, 2 * total * first + size)
        out[at, :] = jnp.dot(move, group, preferred_element_type=jnp.float32).astype(out.dtype)
        copies.append(pltpu.make_async_copy(out.at[at], out_hbm.at[at], sems.at[len(copies)]))
        copies[-1].start()
    for copy in copies:
        copy.wait()


def channel_kernel(
    scale, block, got_ref, order_ref, weight_ref, dir_ref, vis_hbm, beam_ref,
    flat, mixed, turned, across, vis, sems,
):
    sections, chans, pair, inputs = got_ref.shape
    frames = sections * pair // 2
    total = flat.shape[1]
    for c in range(chans):
        flat[:, c * inputs : (c + 1) * inputs] = got_ref[:, c].reshape(2 * frames, inputs)
    for start in range(0, total, block):
        at = slice(start, start + block)
        source = lax.broadcasted_iota(jnp.int32, (total, block), 0)
        chosen = (source == order_ref[:, at]).astype(jnp.bfloat16)
        picked = jnp.dot(flat[...], chosen, preferred_element_type=jnp.float32)
        parts = picked.reshape(sections, 2, pair // 2, block)
        real = parts[:, 0].reshape(frames, block)
        imag = parts[:, 1].reshape(frames, block)
        both = jnp.concatenate([real, imag], axis=0).astype(mixed.dtype)
        mixed[:, at] = both
        turned[:, at] = jnp.concatenate([-imag, real], axis=0).astype(turned.dtype)
        across[at, :] = both.T
    copies = []
    for start in range(0, total, block):
        at = slice(start, start + block)
        end = start + block
        above = jnp.dot(across[:end], mixed[:, at], preferred_element_type=jnp.float32)
        below = jnp.dot(across[start:], turned[:, at], preferred_element_type=jnp.float32)
        row = lax.broadcasted_iota(jnp.int32, (block, block), 0)
        col = lax.broadcasted_iota(jnp.int32, (block, block), 1)
        crossing = jnp.where(col >= row, above[start:], below[:block])
        if start > 0:
            vis[:start, at] = (above[:start] * scale).astype(vis.dtype)
        vis[at, at] = (crossing * scale).astype(vis.dtype)
        if end < total:
            vis[end:, at] = (below[block:] * scale).astype(vis.dtype)
        copies.append(pltpu.make_async_copy(vis.at[:, at], vis_hbm.at[:, at], sems.at[len(copies)]))
        copies[-1].start()
    mix = jnp.dot(weight_ref[...], across[...], preferred_element_type=jnp.float32)
    dirs = mix.shape[0] // 2
    beam_real = mix[:dirs, :frames] - mix[dirs:, frames:]
    beam_imag = mix[:dirs, frames:] + mix[dirs:, :frames]
    formed = jnp.concatenate([beam_real, beam_imag], axis=1).astype(jnp.bfloat16)
    beams = beam_ref.shape[1]
    row = lax.broadcasted_iota(jnp.int32, (dirs, beams), 0)
    chosen = (row == dir_ref[...]).astype(jnp.bfloat16)
    spread = lax.dot_general(chosen, formed, MAJOR, preferred_element_type=jnp.float32)
    beam_ref[0] = spread[:, :frames].astype(beam_ref.dtype)
    beam_ref[1] = spread[:, frames:].astype(beam_ref.dtype)
    for copy in copies:
        copy.wait()


def on_device(voltages, fir_taps, steer, beam_dir, input_order):
    section_count = lax.axis_size("section")
    chan_count = lax.axis_size("chan")
    devices = section_count * chan_count
    spec_dev, inputs_here, frame = voltages.shape
    taps = fir_taps.shape[0]
    lag = taps - 1
    channels = devices
    first = frame // 8
    rows = 2 * channels
    total_inputs = inputs_here * chan_count
    total_frames = spec_dev * section_count
    block = min(512, inputs_here)
    whole = pl.BlockSpec(memory_space=pltpu.VMEM)

    stay = pl.BlockSpec(memory_space=pltpu.HBM)

    def call(kernel, frames, operands, specs, outs, scratch):
        held = frames * inputs_here * frame * voltages.dtype.itemsize
        limit = held + 2 * taps * rows * frame * 2 + (12 << 20)
        return pl.pallas_call(
            functools.partial(kernel, spec_dev, taps, block),
            in_specs=specs,
            out_specs=[whole] * len(outs),
            out_shape=outs,
            scratch_shapes=[
                pltpu.VMEM((frames, inputs_here, frame), voltages.dtype),
                pltpu.SemaphoreType.DMA((frames * inputs_here // block,)),
                *scratch,
            ],
            compiler_params=pltpu.CompilerParams(vmem_limit_bytes=limit),
            cost_estimate=pl.CostEstimate(
                flops=2 * taps * rows * frame * inputs_here * frames,
                bytes_accessed=held,
                transcendentals=0,
            ),
        )(*operands)

    keep = lambda x: pltpu.with_memory_space_constraint(x, pltpu.HBM)
    own, tail, table, ready = call(
        functools.partial(last_frames_kernel, first),
        lag,
        (voltages, keep(fir_taps)),
        [stay, stay],
        [
            jax.ShapeDtypeStruct((lag, rows, inputs_here), jnp.float32),
            jax.ShapeDtypeStruct((lag, rows, inputs_here), jnp.bfloat16),
            jax.ShapeDtypeStruct((taps * rows, frame), jnp.bfloat16),
            jax.ShapeDtypeStruct((PRE, inputs_here, frame), voltages.dtype),
        ],
        [
            pltpu.VMEM(fir_taps.shape, fir_taps.dtype),
            pltpu.SemaphoreType.DMA,
            pltpu.SemaphoreType.DMA((PRE, inputs_here // block)),
        ],
    )
    carried = lax.ppermute(tail, "section", [(i, i + 1) for i in range(section_count - 1)])
    (sums,) = call(
        first_frames_kernel,
        spec_dev - lag,
        (voltages, table, own, ready),
        [stay, whole, whole, whole],
        [jax.ShapeDtypeStruct((spec_dev, rows, inputs_here), jnp.float32)],
        [],
    )
    spectra = pl.pallas_call(
        join_kernel,
        in_specs=[whole] * 2,
        out_specs=pl.BlockSpec(memory_space=pl.ANY),
        out_shape=jax.ShapeDtypeStruct((rows * spec_dev, inputs_here), jnp.bfloat16),
        scratch_shapes=[
            pltpu.VMEM((rows * spec_dev, inputs_here), jnp.bfloat16),
            pltpu.SemaphoreType.DMA((channels // GROUP,)),
        ],
        compiler_params=pltpu.CompilerParams(vmem_limit_bytes=12 << 20),
    )(sums, carried)
    got = lax.all_to_all(
        spectra.reshape(devices, 2 * spec_dev, inputs_here),
        ("section", "chan"),
        split_axis=0,
        concat_axis=0,
        tiled=True,
    ).reshape(section_count, chan_count, 2 * spec_dev, inputs_here)

    channel = lax.axis_index("section") * chan_count + lax.axis_index("chan")
    phase = steer * (first + channel).astype(jnp.float32)
    size = math.sqrt(total_inputs)
    weights = jnp.concatenate([jnp.cos(phase) / size, -jnp.sin(phase) / size], axis=0).astype(
        jnp.bfloat16
    )
    beam_count = beam_dir.shape[0]
    block = min(256, total_inputs)
    lanes = 2 * total_frames
    vis, beams = pl.pallas_call(
        functools.partial(channel_kernel, 1.0 / math.sqrt(total_frames), block),
        in_specs=[whole] * 4,
        out_specs=[pl.BlockSpec(memory_space=pl.ANY), whole],
        out_shape=[
            jax.ShapeDtypeStruct((total_inputs, total_inputs), jnp.bfloat16),
            jax.ShapeDtypeStruct((2, beam_count, total_frames), jnp.bfloat16),
        ],
        scratch_shapes=[
            pltpu.VMEM((lanes, total_inputs), jnp.bfloat16),
            pltpu.VMEM((lanes, total_inputs), jnp.bfloat16),
            pltpu.VMEM((lanes, total_inputs), jnp.bfloat16),
            pltpu.VMEM((total_inputs, lanes), jnp.bfloat16),
            pltpu.VMEM((total_inputs, total_inputs), jnp.bfloat16),
            pltpu.SemaphoreType.DMA((total_inputs // block,)),
        ],
        compiler_params=pltpu.CompilerParams(vmem_limit_bytes=32 << 20),
    )(got, input_order.reshape(1, total_inputs), weights, beam_dir.reshape(1, beam_count))
    return (vis[None], beams[None])


def solution(mesh):
    return jax.shard_map(
        on_device,
        mesh=mesh,
        in_specs=(P("section", "chan", None), P(), P(), P(), P()),
        out_specs=(P(("section", "chan"), None, None), P(("section", "chan"), None, None, None)),
        check_vma=False,
    )
```
